512 devices in a mesh: dp: 32 (over x, y_hi, core), fsdp: 16 (over y_lo, z).
Axes of the slice: x: 4, y: 8 (y_hi: 4, y_lo: 2; y = y_hi * 2 + y_lo), z: 8, core: 2. Of those that a mesh axis runs over, the one named last changes fastest.
Arguments:
- hidden: bfloat16 [4, 2048, 16, 4096], P(None, 'dp', 'fsdp'), may hold values from -6 to 6
- frozen_query_rows: bfloat16 [4, 2048, 16, 2048], P(None, 'dp', 'fsdp'), may hold values from -10 to 10
- output_gradient: bfloat16 [4, 2048, 16, 2048], P(None, 'dp', 'fsdp'), may hold values from -6 to 6
- token_log_ratio: float32 [4, 2048, 16], P(None, 'dp', 'fsdp'), may hold values from -0.15625 to 0.15625
- lengths: int32 [4], replicated, may hold values from 1 to 32768, as said below
- response_win_probability: float32 [4], replicated, may hold values from 0.05 to 0.95
- cached_prompt_keys: bfloat16 [1024, 512], P('fsdp'), may hold values from -7.5 to 7.5
- cached_prompt_values: bfloat16 [1024, 512], P('fsdp'), may hold values from -6 to 6
- adapter_down_factor: bfloat16 [4096, 64], P('fsdp'), may hold values from -0.09375 to 0.09375
- adapter_up_factor: bfloat16 [64, 2048], P(None, 'fsdp'), may hold values from -0.125 to 0.125
- attention_norm_gain: bfloat16 [4096], P('fsdp'), may hold values from 0.5 to 1.5
Outputs:
- grad_down: float32 [4096, 64], P('fsdp')
- grad_up: float32 [64, 2048], P(None, 'fsdp')
- seq_ratio: float32 [4], replicated
The draws below stay inside these ranges and needn't reach their ends.
Inputs may be any that keep to these rules, and one draw needn't show every extreme that they name: The lengths sum to 65472 and the longest is exactly 32768.
All inputs are finite; a program needn't handle non-finite values.
Results may differ from the reference program's by a relative error of at most 0.012.
Values may be sent and summed in bfloat16 or wider, within the bound.
A program may use at most 128 MiB of HBM per device.

```python
import math
import jax
import jax.numpy as jnp
from jax import lax

MODEL_WIDTH = 4096
HEAD_SIZE = 128
QUERY_HEADS = 16
KEY_VALUE_HEADS = 4
ADAPTER_RANK = 64
PROMPT_LENGTH = 1024
RESP = 4
QUERY_COLUMNS = 2048
KW = 512
LPOS = 2048
STRIDE = 16
LMAX = 32768
TOTAL_LEN = 65472
N_DP = 32


def spread_scale(own_key, entries, lower, upper):
    return jnp.exp(jax.random.uniform(own_key, (entries,), jnp.float32, math.log(lower), math.log(upper)))


def draw_lengths(key, part):
    own_key = jax.random.fold_in(key, 4177)
    remaining = TOTAL_LEN - LMAX
    pieces = [jnp.full((1,), LMAX, jnp.int32)]
    left_over = jnp.array(remaining, jnp.int32)
    for piece_index in range(RESP - 2):
        piece_key = jax.random.fold_in(own_key, piece_index)
        others_after = RESP - 2 - piece_index
        amount = jax.random.randint(piece_key, (1,), 1, left_over - others_after + 1, jnp.int32)
        pieces.append(amount)
        left_over = left_over - amount[0]
    pieces.append(left_over.reshape(1))
    joined = jnp.concatenate(pieces, axis=0)
    order = jax.random.permutation(jax.random.fold_in(own_key, 991), RESP)
    return joined[order].astype(jnp.int32)


def draw_frozen_query_rows(key, part):
    own_key = jax.random.fold_in(key, 23)
    full_shape = (RESP, LPOS, STRIDE, QUERY_HEADS, HEAD_SIZE)
    value_vectors = jax.random.truncated_normal(own_key, -4.0, 4.0, full_shape, jnp.float32)
    return value_vectors.reshape(RESP, LPOS, STRIDE, QUERY_HEADS * HEAD_SIZE).astype(jnp.bfloat16)


def draw_cached_prompt_keys(key, part):
    group_key_rows = jax.random.split(jax.random.fold_in(key, 37), 2)
    row_weighting = spread_scale(group_key_rows[0], PROMPT_LENGTH, 0.3, 3.0)[:, None, None]
    value_vectors = jax.random.truncated_normal(group_key_rows[1], -2.5, 2.5, (PROMPT_LENGTH, KEY_VALUE_HEADS, HEAD_SIZE), jnp.float32) * row_weighting
    return value_vectors.reshape(PROMPT_LENGTH, KEY_VALUE_HEADS * HEAD_SIZE).astype(jnp.bfloat16)


def block_levels(key, extent, shards, least, largest):
    factor_of, own = 1.0, jax.random.fold_in(key, 6)
    for dim, shards_of in shards:
        steps = jnp.exp(jax.random.uniform(jax.random.fold_in(own, dim), (shards_of,), jnp.float32, least / len(shards), largest / len(shards)))
        factor_of = factor_of * jnp.repeat(steps, extent[dim] // shards_of).reshape([-1 if axis == dim else 1 for axis in range(len(extent))])
    return factor_of


def bell_draw(key, dims, spread, reach, cuts=(), kind=jnp.bfloat16):
    result = spread * jax.random.normal(key, dims, jnp.float32)
    if cuts:
        result = result * block_levels(key, dims, cuts, -0.22, 0.18)
    return jnp.clip(result, -reach, reach).astype(kind)


def setup_inputs(seed: int = 0) -> dict:
    key_list = jax.random.split(jax.random.key(seed), 12)
    return {
        "hidden": bell_draw(key_list[0], (RESP, LPOS, STRIDE, MODEL_WIDTH), 1.0, 6.0, ((1, 32), (2, 16))),
        "frozen_query_rows": draw_frozen_query_rows(jax.random.fold_in(key_list[11], 71), 0),
        "output_gradient": bell_draw(key_list[2], (RESP, LPOS, STRIDE, QUERY_COLUMNS), 1.0, 6.0, ((1, 32), (2, 16))),
        "token_log_ratio": bell_draw(key_list[3], (RESP, LPOS, STRIDE), 0.01, 0.15625, ((1, 32), (2, 16)), jnp.float32),
        "lengths": draw_lengths(jax.random.fold_in(key_list[11], 71), 0),
        "response_win_probability": jnp.clip(jax.random.uniform(key_list[5], (RESP,), jnp.float32, 0.05, 0.95), 0.05, 0.95),
        "cached_prompt_keys": draw_cached_prompt_keys(jax.random.fold_in(key_list[11], 71), 0),
        "cached_prompt_values": bell_draw(key_list[7], (PROMPT_LENGTH, KW), 1.0, 6.0, ((0, 16),)),
        "adapter_down_factor": bell_draw(key_list[8], (MODEL_WIDTH, ADAPTER_RANK), MODEL_WIDTH ** -0.5, 0.09375, ((0, 16),)),
        "adapter_up_factor": bell_draw(key_list[9], (ADAPTER_RANK, QUERY_COLUMNS), QUERY_COLUMNS ** -0.5, 0.125, ((1, 16),)),
        "attention_norm_gain": jnp.clip(1.0 + 0.1 * jax.random.normal(key_list[10], (MODEL_WIDTH,), jnp.float32), 0.5, 1.5).astype(jnp.bfloat16),
    }


target_scale = 1.0
norm_epsilon = 1e-05

def attend(query_vectors, cotangent, key_rows, value_rows):
    row_count = query_vectors.shape[0]
    queries_per_group = QUERY_HEADS // KEY_VALUE_HEADS
    score_scale = 1.0 / math.sqrt(HEAD_SIZE)
    pieces = []
    for shared_key_head in range(KEY_VALUE_HEADS):
        head_start = shared_key_head * queries_per_group * HEAD_SIZE
        head_stop = head_start + queries_per_group * HEAD_SIZE
        head_query = query_vectors[:, head_start:head_stop].reshape(row_count, queries_per_group, HEAD_SIZE).astype(jnp.float32)
        head_grad = cotangent[:, head_start:head_stop].reshape(row_count, queries_per_group, HEAD_SIZE).astype(jnp.float32)
        head_key = key_rows[:, shared_key_head * HEAD_SIZE:(shared_key_head + 1) * HEAD_SIZE].astype(jnp.float32)
        head_value = value_rows[:, shared_key_head * HEAD_SIZE:(shared_key_head + 1) * HEAD_SIZE].astype(jnp.float32)
        scores = jnp.einsum('nhd,jd->nhj', head_query, head_key) * score_scale
        row_top = lax.optimization_barrier(jnp.max(scores, axis=2, keepdims=True))
        exponent = jnp.exp(scores - row_top)
        row_total = lax.optimization_barrier(jnp.sum(exponent, axis=2, keepdims=True))
        weights = exponent.astype(jnp.bfloat16)
        mixed_out = jnp.einsum('nhj,jd->nhd', weights.astype(jnp.float32), head_value) / row_total
        inner_prod = lax.optimization_barrier(jnp.sum(head_grad * mixed_out, axis=2, keepdims=True))
        grad_prob = jnp.einsum('nhd,jd->nhj', head_grad, head_value)
        grad_score = (weights.astype(jnp.float32) / row_total * (grad_prob - inner_prod)).astype(jnp.bfloat16)
        query_gradient = jnp.einsum('nhj,jd->nhd', grad_score.astype(jnp.float32), head_key) * score_scale
        pieces.append(query_gradient.reshape(row_count, queries_per_group * HEAD_SIZE))
    return jnp.concatenate(pieces, axis=1).astype(jnp.bfloat16)

def reference(hidden, frozen_query_rows, output_gradient, token_log_ratio, lengths, response_win_probability, cached_prompt_keys, cached_prompt_values, adapter_down_factor, adapter_up_factor, attention_norm_gain):
    position = jnp.arange(LPOS, dtype=jnp.int32)[:, None] * STRIDE + jnp.arange(STRIDE, dtype=jnp.int32)[None, :]
    is_valid = position[None, :, :] < lengths[:, None, None]
    seq_ratio = lax.optimization_barrier(jnp.sum(jnp.where(is_valid, token_log_ratio, 0.0), axis=(1, 2)))
    weighting = 2.0 * (seq_ratio - target_scale * (response_win_probability - 0.5)) / RESP
    block_count = RESP * N_DP
    block_rows = LPOS // N_DP * STRIDE
    tokens = hidden.reshape(block_count, block_rows, MODEL_WIDTH)
    base_blocks = frozen_query_rows.reshape(block_count, block_rows, QUERY_COLUMNS)
    upstream = output_gradient.reshape(block_count, block_rows, QUERY_COLUMNS)
    mask_blocks = is_valid.reshape(block_count, block_rows)
    block_weight = jnp.repeat(weighting, N_DP)
    gain_vector = attention_norm_gain.astype(jnp.float32)

    def accumulate(running, block_item):
        total_down, total_up = running
        block_tokens, block_query_start, block_grad, block_mask, block_coef = block_item
        widened = block_tokens.astype(jnp.float32)
        inverse = lax.rsqrt(lax.optimization_barrier(jnp.mean(widened * widened, axis=1, keepdims=True)) + norm_epsilon)
        normed_input = (widened * inverse * gain_vector).astype(jnp.bfloat16)
        lowrank_hidden = jnp.dot(normed_input, adapter_down_factor, preferred_element_type=jnp.float32).astype(jnp.bfloat16)
        query_vectors = (block_query_start.astype(jnp.float32) + jnp.dot(lowrank_hidden, adapter_up_factor, preferred_element_type=jnp.float32)).astype(jnp.bfloat16)
        cotangent = jnp.where(block_mask[:, None], block_coef * block_grad.astype(jnp.float32), 0.0).astype(jnp.bfloat16)
        query_gradient = attend(query_vectors, cotangent, cached_prompt_keys, cached_prompt_values)
        total_up = total_up + jnp.dot(lowrank_hidden.T, query_gradient, preferred_element_type=jnp.float32)
        gradient_lowrank = jnp.dot(query_gradient, adapter_up_factor.T, preferred_element_type=jnp.float32).astype(jnp.bfloat16)
        total_down = total_down + jnp.dot(normed_input.T, gradient_lowrank, preferred_element_type=jnp.float32)
        return ((total_down, total_up), None)
    initial = (jnp.zeros((MODEL_WIDTH, ADAPTER_RANK), jnp.float32), jnp.zeros((ADAPTER_RANK, QUERY_COLUMNS), jnp.float32))
    totals, unused = lax.scan(accumulate, initial, (tokens, base_blocks, upstream, mask_blocks, block_weight))
    return (totals[0], totals[1], seq_ratio)
```

```python
import math

import jax
import jax.numpy as jnp
from jax import lax
from jax.experimental import pallas as pl
from jax.experimental.pallas import tpu as pltpu
from jax.sharding import PartitionSpec as P

MESH = pl.DeviceIdType.MESH
HEAD = 128
HEADS = 16
GROUPS = 4
RANK = 64
WIDTH = 4096
PROMPT = 1024
RESP = 4
ROWS = 256
FS = 16
NZ, NX, NYH = 8, 4, 4
PROWS, PCOLS = 40, 384
EPS = 1e-05
BF, F32 = jnp.bfloat16, jnp.float32


def place():
    dp = lax.axis_index("dp")
    fs = lax.axis_index("fsdp")
    core = lax.rem(dp, 2)
    yh = lax.rem(dp // 2, NYH)
    x = dp // (2 * NYH)
    z = lax.rem(fs, NZ)
    yl = fs // NZ
    return x, yh, core, yl, z


def dev(x, yh, core, yl, z):
    return ((x * NYH + yh) * 2 + core, yl * NZ + z)


def send(src, dst, ssem, rsem, where):
    copy = pltpu.make_async_remote_copy(
        src_ref=src, dst_ref=dst, send_sem=ssem, recv_sem=rsem, device_id=where, device_id_type=MESH
    )
    copy.start()
    return copy


def greet(peers):
    barrier = pltpu.get_barrier_semaphore()
    for where in peers:
        pl.semaphore_signal(barrier, inc=1, device_id=where, device_id_type=MESH)
    pl.semaphore_wait(barrier, len(peers))


CHUNKS = 5


def gather_kernel(
    lengths_ref, tlr_ref, k_ref, v_ref, down_ref, up_ref, gain_ref,
    seq_ref, kv_ref, par_ref,
    kv, par, tot0, tot1, tot2, tot3,
    load_sem, zs_sem, zr_sem, ys_sem, yr_sem, cs_sem, cr_sem, ts_sem, tr_sem, out_sem,
):
    x, yh, core, yl, z = place()
    me = yl * NZ + z
    y = yh * 2 + yl
    other = 1 - core
    loads = []
    for g in range(GROUPS):
        cols = pl.ds(g * HEAD, HEAD)
        for kind, src in ((0, k_ref), (1, v_ref)):
            loads.append(pltpu.make_async_copy(src.at[:, cols], kv.at[kind, g, me], load_sem.at[kind * GROUPS + g]))
    for half in range(2):
        rows = pl.ds(half * 32, 32)
        loads.append(pltpu.make_async_copy(down_ref.at[rows, :], par.at[half, me, pl.ds(0, 32), pl.ds(0, 256)], load_sem.at[8 + 3 * half]))
        loads.append(pltpu.make_async_copy(up_ref.at[rows, :], par.at[half, me, pl.ds(0, 32), pl.ds(256, 128)], load_sem.at[9 + 3 * half]))
        loads.append(pltpu.make_async_copy(gain_ref, par.at[half, me, pl.ds(32, 8), :], load_sem.at[10 + 3 * half]))
    for copy in loads:
        copy.start()

    place_row = lax.broadcasted_iota(jnp.int32, (RESP, 64), 1)
    resp = lax.broadcasted_iota(jnp.int32, (RESP, 64), 0)
    position = (((x * NYH + yh) * 2 + core) * 64 + place_row) * FS + me
    limit = jnp.full((RESP, 64), lengths_ref[0], jnp.int32)
    for r in range(1, RESP):
        limit = jnp.where(resp == r, lengths_ref[r], limit)
    mine = jnp.sum(jnp.where(position < limit, tlr_ref[...], 0.0), axis=1, keepdims=True)
    tot0[core] = jnp.zeros((8, 128), F32)
    tot0[core, pl.ds(0, RESP), :] = jnp.broadcast_to(mine, (RESP, 128))

    peers = [dev(x, yh, other, yl, z)]
    peers += [dev(lax.rem(x + d, NX), yh, core, yl, z) for d in range(1, NX)]
    peers += [dev(x, lax.rem(y + d, 8) // 2, core, lax.rem(lax.rem(y + d, 8), 2), z) for d in range(1, 8)]
    peers += [dev(x, yh, core, yl, lax.rem(z + d, NZ)) for d in range(1, NZ)]
    greet(peers)
    for copy in loads:
        copy.wait()

    right = dev(x, yh, core, yl, lax.rem(z + 1, NZ))
    left = dev(x, yh, core, yl, lax.rem(z + NZ - 1, NZ))
    flip = dev(x, yh, core, 1 - yl, z)
    twin = dev(x, yh, other, yl, z)
    waits = []

    def piece(kind, f, chunk):
        return par.at[kind, f] if chunk == 0 else kv.at[kind, chunk - 1, f]

    def go(where, kind, f, chunk, ssem, rsem):
        ref = piece(kind, f, chunk)
        waits.append(send(ref, ref, ssem, rsem, where))

    def arrive(kind, f, chunk, rsem):
        ref = piece(kind, f, chunk)
        pltpu.make_async_remote_copy(
            src_ref=ref, dst_ref=ref, send_sem=rsem, recv_sem=rsem, device_id=twin, device_id_type=MESH
        ).wait_recv()

    def twin_send(b, zo, chunk, slot):
        go(twin, core, b * NZ + zo, chunk, cs_sem.at[slot, chunk], cr_sem.at[slot, chunk])

    sums = [
        (tot0, 2, core, lambda d: twin, 0),
        (tot1, NX, x, lambda d: dev(lax.rem(x + d, NX), yh, core, yl, z), 1),
        (tot2, 8, y, lambda d: dev(x, lax.rem(y + d, 8) // 2, core, lax.rem(lax.rem(y + d, 8), 2), z), 4),
        (tot3, NZ, z, lambda d: dev(x, yh, core, yl, lax.rem(z + d, NZ)), 11),
    ]

    def sum_start(i):
        buf, n, at, who, base = sums[i]
        return [send(buf.at[at], buf.at[at], ts_sem.at[base + d - 1], tr_sem.at[base + d - 1], who(d)) for d in range(1, n)]

    def sum_end(i, copies):
        buf, n, at, who, base = sums[i]
        for copy in copies:
            copy.wait()
        total = buf[0]
        for j in range(1, n):
            total = total + buf[j]
        return total

    sum_copies = sum_start(0)
    for t in range(CHUNKS + 4):
        for chunk in range(CHUNKS):
            step = t - chunk
            if step == 0:
                go(flip, core, me, chunk, ys_sem.at[chunk], yr_sem.at[chunk])
                for b, side in ((0, right), (1, left)):
                    go(side, core, me, chunk, zs_sem.at[b, 0, 0, chunk], zr_sem.at[b, 0, 0, chunk])
                arrive(core, (1 - yl) * NZ + z, chunk, yr_sem.at[chunk])
                for b, side in ((0, right), (1, left)):
                    go(side, core, (1 - yl) * NZ + z, chunk, zs_sem.at[b, 0, 1, chunk], zr_sem.at[b, 0, 1, chunk])
                twin_send(1 - yl, z, chunk, 1)
            elif 1 <= step <= 4:
                for lane in range(2):
                    b = yl if lane == 0 else 1 - yl
                    for way, side in ((0, right), (1, left)):
                        if step == 4 and (lane != way):
                            continue
                        zo = lax.rem(z + NZ - step, NZ) if way == 0 else lax.rem(z + step, NZ)
                        f = b * NZ + zo
                        arrive(core, f, chunk, zr_sem.at[way, step - 1, lane, chunk])
                        if step < 3 or (step == 3 and lane == way):
                            go(side, core, f, chunk, zs_sem.at[way, step, lane, chunk], zr_sem.at[way, step, lane, chunk])
                        twin_send(b, zo, chunk, 2 + ((step - 1) * 2 + lane) * 2 + way if step < 4 else 14 + lane)
        if t == 1:
            tot1[x] = sum_end(0, sum_copies)
            sum_copies = sum_start(1)
        if t == 3:
            tot2[y] = sum_end(1, sum_copies)
            sum_copies = sum_start(2)
        if t == 5:
            tot3[z] = sum_end(2, sum_copies)
            sum_copies = sum_start(3)
    seq_ref[...] = sum_end(3, sum_copies)
    for copy in waits:
        copy.wait_send()
    for chunk in range(CHUNKS):
        arrive(other, (1 - yl) * NZ + z, chunk, cr_sem.at[1, chunk])
        for step in range(1, 5):
            for lane in range(2):
                b = yl if lane == 0 else 1 - yl
                for way in range(2):
                    if step == 4 and (lane != way):
                        continue
                    zo = lax.rem(z + NZ - step, NZ) if way == 0 else lax.rem(z + step, NZ)
                    slot = 2 + ((step - 1) * 2 + lane) * 2 + way if step < 4 else 14 + lane
                    arrive(other, b * NZ + zo, chunk, cr_sem.at[slot, chunk])
    outs = [pltpu.make_async_copy(kv, kv_ref, out_sem.at[0]), pltpu.make_async_copy(par, par_ref, out_sem.at[1])]
    for copy in outs:
        copy.start()
    for copy in outs:
        copy.wait()


def gather(lengths, tlr, k, v, down_t, up, gain8):
    any_ = pl.BlockSpec(memory_space=pl.ANY)
    vmem = pl.BlockSpec(memory_space=pltpu.VMEM)
    dma = pltpu.SemaphoreType.DMA
    return pl.pallas_call(
        gather_kernel,
        out_shape=(
            jax.ShapeDtypeStruct((8, 128), F32),
            jax.ShapeDtypeStruct((2, GROUPS, FS, 64, HEAD), BF),
            jax.ShapeDtypeStruct((2, FS, PROWS, PCOLS), BF),
        ),
        in_specs=[pl.BlockSpec(memory_space=pltpu.SMEM), vmem, any_, any_, any_, any_, any_],
        out_specs=(vmem, any_, any_),
        scratch_shapes=[
            pltpu.VMEM((2, GROUPS, FS, 64, HEAD), BF),
            pltpu.VMEM((2, FS, PROWS, PCOLS), BF),
            pltpu.VMEM((2, 8, 128), F32),
            pltpu.VMEM((NX, 8, 128), F32),
            pltpu.VMEM((8, 8, 128), F32),
            pltpu.VMEM((NZ, 8, 128), F32),
            dma((14,)),
            dma((2, 4, 2, CHUNKS)),
            dma((2, 4, 2, CHUNKS)),
            dma((CHUNKS,)),
            dma((CHUNKS,)),
            dma((16, CHUNKS)),
            dma((16, CHUNKS)),
            dma((18,)),
            dma((18,)),
            dma((2,)),
        ],
        compiler_params=pltpu.CompilerParams(collective_id=0, has_side_effects=True),
        name="gather",
    )(lengths, tlr, k, v, down_t, up, gain8)


NT = (((1,), (1,)), ((), ()))
TN = (((0,), (0,)), ((), ()))


def mm(a, b, dims=(((1,), (0,)), ((), ()))):
    return lax.dot_general(a, b, dims, preferred_element_type=F32)


def math_kernel(
    lengths_ref, win_ref, dp_ref, seq_ref, hidden_ref, frozen_ref, grad_ref, kv_ref, par_ref,
    out_ref,
    normed, low_ref, low32, inv_ref, coef_ref, glow_ref,
):
    dp, fs = dp_ref[0], dp_ref[1]
    scale = 1.0 / math.sqrt(HEAD)
    place_row = lax.broadcasted_iota(jnp.int32, (64, 1), 0)
    position = (dp * 64 + place_row) * FS + fs
    for r in range(RESP):
        seq = seq_ref[pl.ds(r, 1), pl.ds(0, 1)]
        weight = 2.0 * (seq - (win_ref[r] - 0.5)) / RESP
        coef_ref[pl.ds(r * 64, 64), :] = jnp.where(position < lengths_ref[r], jnp.broadcast_to(weight, (64, 1)), 0.0) * scale

    square = jnp.zeros((ROWS, 256), F32)
    for f in range(FS):
        part = hidden_ref[:, pl.ds(f * 256, 256)].astype(F32)
        square = square + part * part
    inv_ref[...] = lax.rsqrt(jnp.sum(square, axis=1, keepdims=True) * (1.0 / WIDTH) + EPS)
    low32[...] = jnp.zeros_like(low32)

    def norm_step(f, carry):
        cols = pl.ds(pl.multiple_of(f * 256, 256), 256)
        part = hidden_ref[:, cols].astype(F32)
        gain = par_ref[0, f, pl.ds(32, 8), pl.ds(0, 256)].astype(F32)[0:1]
        value = (part * inv_ref[...] * gain).astype(BF)
        normed[:, cols] = value
        down = par_ref[:, f, pl.ds(0, 32), pl.ds(0, 256)].reshape(RANK, 256)
        low32[...] += mm(value, down, NT)
        return carry

    lax.fori_loop(0, FS, norm_step, 0)
    low_ref[...] = low32[...].astype(BF)
    glow_ref[...] = jnp.zeros_like(glow_ref)

    def head_step(h, carry):
        g = h // (HEADS // GROUPS)
        cols = pl.ds(pl.multiple_of(h * HEAD, HEAD), HEAD)
        up = par_ref[:, h, pl.ds(0, 32), pl.ds(256, HEAD)].reshape(RANK, HEAD)
        query = (frozen_ref[:, cols].astype(F32) + mm(low_ref[...], up)).astype(BF)
        keys = kv_ref[0, g].reshape(PROMPT, HEAD)
        values = kv_ref[1, g].reshape(PROMPT, HEAD)
        scores = mm(query, keys, NT)
        top = jnp.max(scores, axis=1, keepdims=True)
        c = scale * math.log2(math.e)
        expo = jnp.exp2((scores - top) * c)
        total = jnp.sum(expo, axis=1, keepdims=True)
        weights = expo.astype(BF)
        grad_prob = mm(grad_ref[:, cols], values, NT)
        wide = weights.astype(F32)
        inner = jnp.sum(wide * grad_prob, axis=1, keepdims=True) / total
        grad_score = (wide * (grad_prob - inner)).astype(BF)
        grad_query = (mm(grad_score, keys) * (coef_ref[...] / total)).astype(BF)
        glow_ref[...] += mm(grad_query, up, NT)
        out_ref[:, :, h, :, pl.ds(256, HEAD)] = mm(low_ref[...], grad_query, TN).astype(BF).reshape(2, NX, 8, HEAD)
        return carry

    lax.fori_loop(0, HEADS, head_step, 0)
    grad_low = glow_ref[...].astype(BF)

    def down_step(f, carry):
        cols = pl.ds(pl.multiple_of(f * 256, 256), 256)
        out_ref[:, :, f, :, pl.ds(0, 256)] = mm(grad_low, normed[:, cols], TN).astype(BF).reshape(2, NX, 8, 256)
        return carry

    lax.fori_loop(0, FS, down_step, 0)


def local_math(lengths, win, dp_fs, seq, hidden, frozen, grad, kv, par):
    smem = pl.BlockSpec(memory_space=pltpu.SMEM)
    vmem = pl.BlockSpec(memory_space=pltpu.VMEM)
    return pl.pallas_call(
        math_kernel,
        out_shape=jax.ShapeDtypeStruct((2, NX, FS, 8, PCOLS), BF),
        in_specs=[smem, smem, smem] + [vmem] * 6,
        out_specs=vmem,
        scratch_shapes=[
            pltpu.VMEM((ROWS, WIDTH), BF),
            pltpu.VMEM((ROWS, RANK), BF),
            pltpu.VMEM((ROWS, RANK), F32),
            pltpu.VMEM((ROWS, 1), F32),
            pltpu.VMEM((ROWS, 1), F32),
            pltpu.VMEM((ROWS, RANK), F32),
        ],
        compiler_params=pltpu.CompilerParams(vmem_limit_bytes=48 * 1024 * 1024),
        name="local_math",
    )(lengths, win, dp_fs, seq, hidden, frozen, grad, kv, par)


def reduce_kernel(
    part_ref, down_out, up_out,
    r0, s0, r1, s1, r2, s2, r3, s4,
    sem0s, sem0r, sem1s, sem1r, sem2s, sem2r, sem3s, sem3r, sem4s, sem4r,
):
    x, yh, core, yl, z = place()
    y = yh * 2 + yl
    other = 1 - core
    twin = dev(x, yh, other, yl, z)
    xs = [dev(lax.rem(x + d, NX), yh, core, yl, z) for d in range(1, NX)]
    xo = [dev(lax.rem(x + d, NX), yh, other, yl, z) for d in range(1, NX)]
    ys = [lax.rem(y + d, 8) for d in range(1, 8)]
    zs = [lax.rem(z + d, NZ) for d in range(1, NZ)]
    ydev = [dev(x, n // 2, core, lax.rem(n, 2), z) for n in ys]
    zdev = [dev(x, yh, core, yl, n) for n in zs]
    greet([twin] + xs + xo + ydev + zdev)

    copies = []
    for i in range(NX):
        copies.append(send(part_ref.at[other, i], r0.at[i], sem0s.at[i], sem0r.at[i], twin))
    steps = []
    for i in range(NX):
        copies[i].wait_recv()
        s0[i] = (part_ref[core, i].astype(F32) + r0[i].astype(F32)).astype(BF)
    for d in range(1, NX):
        steps.append(send(s0.at[lax.rem(x + d, NX)], r1.at[d - 1], sem1s.at[d - 1], sem1r.at[d - 1], xs[d - 1]))
    for copy in steps:
        copy.wait_recv()
    total = s0[x].astype(F32)
    for d in range(1, NX):
        total = total + r1[d - 1].astype(F32)
    s1[...] = total.astype(BF).reshape(2, NZ, 8, PCOLS)
    copies += steps
    steps = []
    for d in range(1, NZ):
        steps.append(send(s1.at[:, zs[d - 1]], r2.at[d - 1], sem2s.at[d - 1], sem2r.at[d - 1], zdev[d - 1]))
    total = s1[:, z].astype(F32)
    for d in range(1, NZ):
        steps[d - 1].wait_recv()
        total = total + r2[d - 1].astype(F32)
    s2[...] = total.astype(BF)
    copies += steps
    steps = []
    for d in range(1, 8):
        steps.append(send(s2.at[lax.rem(ys[d - 1], 2)], r3.at[y], sem3s.at[d - 1], sem3r.at[d - 1], ydev[d - 1]))
    r3[y] = s2[yl]
    for copy in steps:
        copy.wait_recv()
    total = r3[0].astype(F32)
    for j in range(1, 8):
        total = total + r3[j].astype(F32)
    copies += steps
    s4[core, x] = total
    steps = []
    for d, where in enumerate([twin] + xs + xo):
        steps.append(send(s4.at[core, x], s4.at[core, x], sem4s.at[d], sem4r.at[d], where))
    for copy in steps:
        copy.wait_recv()
    whole = s4[...].reshape(RANK, PCOLS)
    down_out[...] = whole[:, 0:256]
    up_out[...] = whole[:, 256:384]
    for copy in copies + steps:
        copy.wait_send()


def reduce(part):
    vmem = pl.BlockSpec(memory_space=pltpu.VMEM)
    dma = pltpu.SemaphoreType.DMA
    return pl.pallas_call(
        reduce_kernel,
        out_shape=(jax.ShapeDtypeStruct((RANK, 256), F32), jax.ShapeDtypeStruct((RANK, HEAD), F32)),
        in_specs=[vmem],
        out_specs=(vmem, vmem),
        scratch_shapes=[
            pltpu.VMEM((NX, FS, 8, PCOLS), BF),
            pltpu.VMEM((NX, FS, 8, PCOLS), BF),
            pltpu.VMEM((NX - 1, FS, 8, PCOLS), BF),
            pltpu.VMEM((2, NZ, 8, PCOLS), BF),
            pltpu.VMEM((NZ - 1, 2, 8, PCOLS), BF),
            pltpu.VMEM((2, 8, PCOLS), BF),
            pltpu.VMEM((8, 8, PCOLS), BF),
            pltpu.VMEM((2, NX, 8, PCOLS), F32),
            dma((NX,)), dma((NX,)), dma((3,)), dma((3,)), dma((7,)), dma((7,)), dma((7,)), dma((7,)), dma((7,)), dma((7,)),
        ],
        compiler_params=pltpu.CompilerParams(collective_id=1, has_side_effects=True),
        name="reduce",
    )(part)


def body(
    hidden,
    frozen_query_rows,
    output_gradient,
    token_log_ratio,
    lengths,
    response_win_probability,
    cached_prompt_keys,
    cached_prompt_values,
    adapter_down_factor,
    adapter_up_factor,
    attention_norm_gain,
):
    gain8 = jnp.broadcast_to(jnp.pad(attention_norm_gain, (0, PCOLS - 256))[None, :], (8, PCOLS))
    seq, kv, par = gather(
        lengths,
        token_log_ratio.reshape(RESP, 64),
        cached_prompt_keys,
        cached_prompt_values,
        adapter_down_factor.T,
        adapter_up_factor,
        gain8,
    )
    dp_fs = jnp.stack([lax.axis_index("dp"), lax.axis_index("fsdp")]).astype(jnp.int32)
    part = local_math(
        lengths,
        response_win_probability,
        dp_fs,
        seq,
        hidden.reshape(ROWS, WIDTH),
        frozen_query_rows.reshape(ROWS, HEADS * HEAD),
        output_gradient.reshape(ROWS, HEADS * HEAD),
        kv,
        par,
    )
    grad_down_t, grad_up = reduce(part)
    return grad_down_t.T, grad_up, seq[0:RESP, 0]


def solution(mesh):
    in_specs = (
        P(None, "dp", "fsdp", None),
        P(None, "dp", "fsdp", None),
        P(None, "dp", "fsdp", None),
        P(None, "dp", "fsdp"),
        P(),
        P(),
        P("fsdp", None),
        P("fsdp", None),
        P("fsdp", None),
        P(None, "fsdp"),
        P("fsdp"),
    )
    out_specs = (P("fsdp", None), P(None, "fsdp"), P())
    return jax.shard_map(body, mesh=mesh, in_specs=in_specs, out_specs=out_specs, check_vma=False)
```

```python
import math

import jax
import jax.numpy as jnp
from jax import lax
from jax.experimental import pallas as pl
from jax.experimental.pallas import tpu as pltpu
from jax.sharding import PartitionSpec as P

MESH = pl.DeviceIdType.MESH
HEAD = 128
HEADS = 16
GROUPS = 4
RANK = 64
WIDTH = 4096
PROMPT = 1024
RESP = 4
ROWS = 256
FS = 16
NZ, NX, NYH = 8, 4, 4
PCOLS = 384
EPS = 1e-05
BF, F32 = jnp.bfloat16, jnp.float32


def place():
    dp = lax.axis_index("dp")
    fs = lax.axis_index("fsdp")
    core = lax.rem(dp, 2)
    yh = lax.rem(dp // 2, NYH)
    x = dp // (2 * NYH)
    z = lax.rem(fs, NZ)
    yl = fs // NZ
    return x, yh, core, yl, z


def dev(x, yh, core, yl, z):
    return ((x * NYH + yh) * 2 + core, yl * NZ + z)


def send(src, dst, ssem, rsem, where):
    copy = pltpu.make_async_remote_copy(
        src_ref=src, dst_ref=dst, send_sem=ssem, recv_sem=rsem, device_id=where, device_id_type=MESH
    )
    copy.start()
    return copy


def greet(peers):
    barrier = pltpu.get_barrier_semaphore()
    for where in peers:
        pl.semaphore_signal(barrier, inc=1, device_id=where, device_id_type=MESH)
    pl.semaphore_wait(barrier, len(peers))


NT = (((1,), (1,)), ((), ()))
TN = (((0,), (0,)), ((), ()))
PER = HEADS // GROUPS
SCALE = 1.0 / math.sqrt(HEAD)


def mm(a, b, dims=(((1,), (0,)), ((), ()))):
    return lax.dot_general(a, b, dims, preferred_element_type=F32)


def step_kernel(
    lengths_ref, win_ref, tlr_ref, k_ref, v_ref, down_ref, up_ref, gain_ref, hidden_hbm, frozen_hbm, grad_hbm,
    seq_out, down_out, up_out,
    kv, par, gains, hidden, frozen, grad, normed, low_ref, low32, inv_ref, coef_ref, glow_ref,
    tot1, tot2, part, r0, s0, r1, s1, r2, s2, r3, s4,
    load_sem, big_sem, as_sem, ar_sem, gs_sem, gr_sem, cs_sem, cr_sem, t1s, t1r, t2s, t2r,
    sem0s, sem0r, sem1s, sem1r, sem2s, sem2r, sem3s, sem3r, sem4s, sem4r,
):
    x, yh, core, yl, z = place()
    me = yl * NZ + z
    y = yh * 2 + yl
    spot = lax.axis_index("dp")
    other = 1 - core
    twin = dev(x, yh, other, yl, z)
    hops = [(d, e) for d in (0, 1, 7, 2, 6, 3, 5, 4) for e in (0, 1) if (d, e) != (0, 0)]
    fs_at = [(lax.rem(z + d, NZ), lax.rem(yl + e, 2)) for d, e in hops]
    fs_from = [(lax.rem(z + NZ - d, NZ), lax.rem(yl + e, 2)) for d, e in hops]
    fs_dev = [dev(x, yh, core, b, a) for a, b in fs_at]
    dp_dev = [(lax.rem(spot + d, 32), me) for d in range(1, 32)]
    xs = [dev(lax.rem(x + d, NX), yh, core, yl, z) for d in range(1, NX)]
    xo = [dev(lax.rem(x + d, NX), yh, other, yl, z) for d in range(1, NX)]
    ys = [lax.rem(y + d, 8) for d in range(1, 8)]
    zs = [lax.rem(z + d, NZ) for d in range(1, NZ)]
    y_dev = [dev(x, n // 2, core, lax.rem(n, 2), z) for n in ys]
    z_dev = [dev(x, yh, core, yl, n) for n in zs]
    across = [dev(x, lax.rem(yh + d, NYH), core, 1 - yl, z) for d in range(1, NYH)]

    barrier = pltpu.get_barrier_semaphore()
    greeted = fs_dev + dp_dev + across
    for where in greeted:
        pl.semaphore_signal(barrier, inc=1, device_id=where, device_id_type=MESH)

    rows = pl.ds(pl.multiple_of(core * 32, 32), 32)
    loads = [
        pltpu.make_async_copy(down_ref.at[rows, :], par.at[core, me, :, pl.ds(0, 256)], load_sem.at[0]),
        pltpu.make_async_copy(up_ref.at[rows, :], par.at[core, me, :, pl.ds(256, HEAD)], load_sem.at[1]),
        pltpu.make_async_copy(gain_ref, gains.at[me], load_sem.at[2]),
    ]
    for copy in loads:
        copy.start()
    for kind, src in ((0, k_ref), (1, v_ref)):

        @pl.when(core == kind)
        def _():
            for g in range(GROUPS):
                pltpu.make_async_copy(src.at[:, pl.ds(g * HEAD, HEAD)], kv.at[kind, g, me], load_sem.at[3 + g]).start()

    bigs = [
        pltpu.make_async_copy(hidden_hbm, hidden, big_sem.at[0]),
        pltpu.make_async_copy(frozen_hbm, frozen, big_sem.at[1]),
        pltpu.make_async_copy(grad_hbm, grad, big_sem.at[2]),
    ]
    for copy in bigs:
        copy.start()

    place_row = lax.broadcasted_iota(jnp.int32, (RESP, 64), 1)
    resp = lax.broadcasted_iota(jnp.int32, (RESP, 64), 0)
    position = (spot * 64 + place_row) * FS + me
    limit = jnp.full((RESP, 64), lengths_ref[0], jnp.int32)
    for r in range(1, RESP):
        limit = jnp.where(resp == r, lengths_ref[r], limit)
    mine = jnp.sum(jnp.where(position < limit, tlr_ref[...], 0.0), axis=1, keepdims=True)
    tot1[me] = jnp.concatenate([jnp.broadcast_to(mine, (RESP, 128)), jnp.zeros((8 - RESP, 128), F32)], axis=0)

    for copy in loads:
        copy.wait()
    for g in range(GROUPS):
        pltpu.make_async_copy(k_ref.at[:, pl.ds(g * HEAD, HEAD)], kv.at[core, g, me], load_sem.at[3 + g]).wait()
    pl.semaphore_wait(barrier, len(greeted))

    sent = []
    for i, where in enumerate(fs_dev):
        sent.append(send(gains.at[me], gains.at[me], gs_sem.at[i], gr_sem.at[i], where))
    for i, where in enumerate(fs_dev):
        sent.append(send(par.at[core, me], par.at[core, me], as_sem.at[GROUPS, i], ar_sem.at[GROUPS, i], where))
    for i, where in enumerate(fs_dev):
        sent.append(send(tot1.at[me], tot1.at[me], t1s.at[i], t1r.at[i], where))
    for g in range(GROUPS):
        for i, where in enumerate(fs_dev):
            sent.append(send(kv.at[core, g, me], kv.at[core, g, me], as_sem.at[g, i], ar_sem.at[g, i], where))

    def landed(ref, sem):
        pltpu.make_async_remote_copy(
            src_ref=ref, dst_ref=ref, send_sem=sem, recv_sem=sem, device_id=twin, device_id_type=MESH
        ).wait_recv()

    def origin(i):
        a, b = fs_from[i]
        return b * NZ + a

    bigs[0].wait()
    square = jnp.zeros((ROWS, 256), F32)
    for f in range(FS):
        block = hidden[:, pl.ds(f * 256, 256)].astype(F32)
        square = square + block * block
    inv_ref[...] = lax.rsqrt(jnp.sum(square, axis=1, keepdims=True) * (1.0 / WIDTH) + EPS)
    low32[...] = jnp.zeros_like(low32)
    for i in range(len(fs_dev)):
        landed(gains.at[origin(i)], gr_sem.at[i])

    def norm_step(f, carry):
        gain = gains[f].astype(F32)
        for half in range(2):
            cols = pl.ds(pl.multiple_of(f * 256 + half * 128, 128), 128)
            normed[:, cols] = (hidden[:, cols].astype(F32) * inv_ref[...] * gain[half : half + 1]).astype(BF)
        return carry

    lax.fori_loop(0, FS, norm_step, 0)

    for i in range(len(fs_dev)):
        landed(tot1.at[origin(i)], t1r.at[i])
    total = tot1[0]
    for j in range(1, FS):
        total = total + tot1[j]
    tot2[spot] = total
    for d in range(31):
        sent.append(send(tot2.at[spot], tot2.at[spot], t2s.at[d], t2r.at[d], dp_dev[d]))

    for i in range(len(fs_dev)):
        landed(par.at[core, origin(i)], ar_sem.at[GROUPS, i])
    swap = send(par.at[core], par.at[core], cs_sem.at[GROUPS], cr_sem.at[GROUPS], twin)
    sent.append(swap)
    for i in range(len(fs_dev)):
        landed(kv.at[core, 0, origin(i)], ar_sem.at[0, i])
    first = send(kv.at[core, 0], kv.at[core, 0], cs_sem.at[0], cr_sem.at[0], twin)
    landed(par.at[other], cr_sem.at[GROUPS])

    def low_step(f, carry):
        cols = pl.ds(pl.multiple_of(f * 256, 256), 256)
        low32[...] += mm(normed[:, cols], par[:, f, :, pl.ds(0, 256)].reshape(RANK, 256), NT)
        return carry

    lax.fori_loop(0, FS, low_step, 0)
    low_ref[...] = low32[...].astype(BF)
    glow_ref[...] = jnp.zeros_like(glow_ref)

    for d in range(31):
        landed(tot2.at[lax.rem(spot + 31 - d, 32)], t2r.at[d])
    total = tot2[0]
    for j in range(1, 32):
        total = total + tot2[j]
    seq_out[...] = total
    row = lax.broadcasted_iota(jnp.int32, (64, 1), 0)
    position = (spot * 64 + row) * FS + me
    for r in range(RESP):
        weight = 2.0 * (total[r : r + 1, 0:1] - (win_ref[r] - 0.5)) / RESP
        coef_ref[pl.ds(r * 64, 64), :] = jnp.where(position < lengths_ref[r], jnp.broadcast_to(weight, (64, 1)), 0.0) * SCALE
    bigs[1].wait()
    bigs[2].wait()

    def group_step(g, carry):
        @pl.when(g < GROUPS - 1)
        def _():
            for i in range(len(fs_dev)):
                landed(kv.at[core, g + 1, origin(i)], ar_sem.at[g + 1, i])
            send(kv.at[core, g + 1], kv.at[core, g + 1], cs_sem.at[g + 1], cr_sem.at[g + 1], twin)

        landed(kv.at[other, g], cr_sem.at[g])
        ups, queries, grads = [], [], []
        for a in range(PER):
            h = g * PER + a
            cols = pl.ds(pl.multiple_of(h * HEAD, HEAD), HEAD)
            ups.append(par[:, h, :, pl.ds(256, HEAD)].reshape(RANK, HEAD))
            queries.append((frozen[:, cols].astype(F32) + mm(low_ref[...], ups[a])).astype(BF))
            grads.append(grad[:, cols])
        keys = kv[0, g].reshape(PROMPT, HEAD)
        values = kv[1, g].reshape(PROMPT, HEAD)
        scores = mm(jnp.concatenate(queries, axis=0), keys, NT)
        top = jnp.max(scores, axis=1, keepdims=True)
        expo = jnp.exp2((scores - top) * (SCALE * math.log2(math.e)))
        row_total = jnp.sum(expo, axis=1, keepdims=True)
        weights = expo.astype(BF)
        grad_prob = mm(jnp.concatenate(grads, axis=0), values, NT)
        wide = weights.astype(F32)
        inner = jnp.sum(wide * grad_prob, axis=1, keepdims=True) / row_total
        grad_score = (wide * (grad_prob - inner)).astype(BF)
        coef = jnp.concatenate([coef_ref[...]] * PER, axis=0)
        grad_query = (mm(grad_score, keys) * (coef / row_total)).astype(BF)
        for a in range(PER):
            h = g * PER + a
            block = grad_query[a * ROWS : (a + 1) * ROWS]
            glow_ref[...] += mm(block, ups[a], NT)
            part[:, :, h, :, pl.ds(256, HEAD)] = mm(low_ref[...], block, TN).astype(BF).reshape(2, NX, 8, HEAD)
        return carry

    lax.fori_loop(0, GROUPS, group_step, 0)
    grad_low = glow_ref[...].astype(BF)

    pieces = 4
    size = FS // pieces
    swaps, steps = [], []

    def pass_x(p):
        blocks = pl.ds(p * size, size)
        swaps[p].wait_recv()
        s0[:, blocks] = (part[core, :, blocks].astype(F32) + r0[:, blocks].astype(F32)).astype(BF)
        for d in range(1, NX):
            steps.append(send(s0.at[lax.rem(x + d, NX), blocks], r1.at[d - 1, blocks], sem1s.at[p, d - 1], sem1r.at[p, d - 1], xs[d - 1]))

    for p in range(pieces):
        for f in range(p * size, (p + 1) * size):
            part[:, :, f, :, pl.ds(0, 256)] = mm(grad_low, normed[:, pl.ds(f * 256, 256)], TN).astype(BF).reshape(2, NX, 8, 256)
        blocks = pl.ds(p * size, size)
        swaps.append(send(part.at[other, :, blocks], r0.at[:, blocks], sem0s.at[p], sem0r.at[p], twin))
        if p:
            pass_x(p - 1)
    pass_x(pieces - 1)
    for copy in steps:
        copy.wait_recv()
    sum_x = s0[x].astype(F32)
    for d in range(1, NX):
        sum_x = sum_x + r1[d - 1].astype(F32)
    s1[...] = sum_x.astype(BF).reshape(2, NZ, 8, PCOLS)
    sent += swaps + steps
    steps = []
    for d in range(1, NZ):
        steps.append(send(s1.at[:, zs[d - 1]], r2.at[d - 1], sem2s.at[d - 1], sem2r.at[d - 1], z_dev[d - 1]))
    sum_z = s1[:, z].astype(F32)
    for d in range(1, NZ):
        steps[d - 1].wait_recv()
        sum_z = sum_z + r2[d - 1].astype(F32)
    s2[...] = sum_z.astype(BF)
    sent += steps
    steps = []
    for d in range(1, 8):
        steps.append(send(s2.at[lax.rem(ys[d - 1], 2)], r3.at[y], sem3s.at[d - 1], sem3r.at[d - 1], y_dev[d - 1]))
    r3[y] = s2[yl]
    for copy in steps:
        copy.wait_recv()
    sum_y = r3[0].astype(F32)
    for j in range(1, 8):
        sum_y = sum_y + r3[j].astype(F32)
    sent += steps
    s4[core, x] = sum_y
    steps = []
    for d, where in enumerate([twin] + xs + xo):
        steps.append(send(s4.at[core, x], s4.at[core, x], sem4s.at[d], sem4r.at[d], where))
    for copy in steps:
        copy.wait_recv()
    whole = s4[...].reshape(RANK, PCOLS)
    down_out[...] = whole[:, 0:256]
    up_out[...] = whole[:, 256:384]
    for copy in sent + steps:
        copy.wait_send()
    for g in range(GROUPS):
        pltpu.make_async_remote_copy(
            src_ref=kv.at[core, g], dst_ref=kv.at[core, g], send_sem=cs_sem.at[g], recv_sem=cr_sem.at[g],
            device_id=twin, device_id_type=MESH,
        ).wait_send()


def step(*args):
    any_ = pl.BlockSpec(memory_space=pl.ANY)
    vmem = pl.BlockSpec(memory_space=pltpu.VMEM)
    smem = pl.BlockSpec(memory_space=pltpu.SMEM)
    dma = pltpu.SemaphoreType.DMA
    wide = HEADS * HEAD
    return pl.pallas_call(
        step_kernel,
        out_shape=(
            jax.ShapeDtypeStruct((8, 128), F32),
            jax.ShapeDtypeStruct((RANK, 256), F32),
            jax.ShapeDtypeStruct((RANK, HEAD), F32),
        ),
        in_specs=[smem, smem, vmem] + [any_] * 8,
        out_specs=(vmem, vmem, vmem),
        scratch_shapes=[
            pltpu.VMEM((2, GROUPS, FS, 64, HEAD), BF),
            pltpu.VMEM((2, FS, 32, PCOLS), BF),
            pltpu.VMEM((FS, 2, 128), BF),
            pltpu.VMEM((ROWS, WIDTH), BF),
            pltpu.VMEM((ROWS, wide), BF),
            pltpu.VMEM((ROWS, wide), BF),
            pltpu.VMEM((ROWS, WIDTH), BF),
            pltpu.VMEM((ROWS, RANK), BF),
            pltpu.VMEM((ROWS, RANK), F32),
            pltpu.VMEM((ROWS, 1), F32),
            pltpu.VMEM((ROWS, 1), F32),
            pltpu.VMEM((ROWS, RANK), F32),
            pltpu.VMEM((FS, 8, 128), F32),
            pltpu.VMEM((32, 8, 128), F32),
            pltpu.VMEM((2, NX, FS, 8, PCOLS), BF),
            pltpu.VMEM((NX, FS, 8, PCOLS), BF),
            pltpu.VMEM((NX, FS, 8, PCOLS), BF),
            pltpu.VMEM((NX - 1, FS, 8, PCOLS), BF),
            pltpu.VMEM((2, NZ, 8, PCOLS), BF),
            pltpu.VMEM((NZ - 1, 2, 8, PCOLS), BF),
            pltpu.VMEM((2, 8, PCOLS), BF),
            pltpu.VMEM((8, 8, PCOLS), BF),
            pltpu.VMEM((2, NX, 8, PCOLS), F32),
            dma((7,)), dma((3,)),
            dma((GROUPS + 1, 15)), dma((GROUPS + 1, 15)),
            dma((15,)), dma((15,)),
            dma((GROUPS + 1,)), dma((GROUPS + 1,)),
            dma((15,)), dma((15,)), dma((31,)), dma((31,)),
            dma((4,)), dma((4,)), dma((4, 3)), dma((4, 3)),
            dma((7,)), dma((7,)), dma((7,)), dma((7,)), dma((7,)), dma((7,)),
        ],
        compiler_params=pltpu.CompilerParams(collective_id=0, has_side_effects=True, vmem_limit_bytes=60 * 1024 * 1024),
        name="step",
    )(*args)


def body(
    hidden,
    frozen_query_rows,
    output_gradient,
    token_log_ratio,
    lengths,
    response_win_probability,
    cached_prompt_keys,
    cached_prompt_values,
    adapter_down_factor,
    adapter_up_factor,
    attention_norm_gain,
):
    seq, grad_down_t, grad_up = step(
        lengths,
        response_win_probability,
        token_log_ratio.reshape(RESP, 64),
        cached_prompt_keys,
        cached_prompt_values,
        adapter_down_factor.T,
        adapter_up_factor,
        attention_norm_gain.reshape(2, 128),
        hidden.reshape(ROWS, WIDTH),
        frozen_query_rows.reshape(ROWS, HEADS * HEAD),
        output_gradient.reshape(ROWS, HEADS * HEAD),
    )
    return grad_down_t.T, grad_up, seq[0:RESP, 0]


def solution(mesh):
    in_specs = (
        P(None, "dp", "fsdp", None),
        P(None, "dp", "fsdp", None),
        P(None, "dp", "fsdp", None),
        P(None, "dp", "fsdp"),
        P(),
        P(),
        P("fsdp", None),
        P("fsdp", None),
        P("fsdp", None),
        P(None, "fsdp"),
        P("fsdp"),
    )
    out_specs = (P("fsdp", None), P(None, "fsdp"), P())
    return jax.shard_map(body, mesh=mesh, in_specs=in_specs, out_specs=out_specs, check_vma=False)
```

```python
import math

import jax
import jax.numpy as jnp
from jax import lax
from jax.experimental import pallas as pl
from jax.experimental.pallas import tpu as pltpu
from jax.sharding import PartitionSpec as P

MESH = pl.DeviceIdType.MESH
HEAD = 128
HEADS = 16
GROUPS = 4
RANK = 64
WIDTH = 4096
PROMPT = 1024
RESP = 4
ROWS = 256
FS = 16
NZ, NX, NYH = 8, 4, 4
PCOLS = 384
EPS = 1e-05
BF, F32 = jnp.bfloat16, jnp.float32


def place():
    dp = lax.axis_index("dp")
    fs = lax.axis_index("fsdp")
    core = lax.rem(dp, 2)
    yh = lax.rem(dp // 2, NYH)
    x = dp // (2 * NYH)
    z = lax.rem(fs, NZ)
    yl = fs // NZ
    return x, yh, core, yl, z


def dev(x, yh, core, yl, z):
    return ((x * NYH + yh) * 2 + core, yl * NZ + z)


def send(src, dst, ssem, rsem, where):
    copy = pltpu.make_async_remote_copy(
        src_ref=src, dst_ref=dst, send_sem=ssem, recv_sem=rsem, device_id=where, device_id_type=MESH
    )
    copy.start()
    return copy


def greet(peers):
    barrier = pltpu.get_barrier_semaphore()
    for where in peers:
        pl.semaphore_signal(barrier, inc=1, device_id=where, device_id_type=MESH)
    pl.semaphore_wait(barrier, len(peers))


NT = (((1,), (1,)), ((), ()))
TN = (((0,), (0,)), ((), ()))
PER = HEADS // GROUPS
SCALE = 1.0 / math.sqrt(HEAD)


def mm(a, b, dims=(((1,), (0,)), ((), ()))):
    return lax.dot_general(a, b, dims, preferred_element_type=F32)


def step_kernel(
    lengths_ref, win_ref, tlr_ref, k_ref, v_ref, down_ref, up_ref, gain_ref, hidden_hbm, frozen_hbm, grad_hbm,
    seq_out, down_out, up_out,
    kv, par, gains, hidden, frozen, grad, normed, low_ref, low32, inv_ref, coef_ref, glow_ref,
    tot1, tot2, part, r0, s0, r1, s1, r2, s2, r3, s4,
    load_sem, big_sem, as_sem, ar_sem, fs_sem, fr_sem, gs_sem, gr_sem, cs_sem, cr_sem, t1s, t1r, t2s, t2r,
    sem0s, sem0r, sem1s, sem1r, sem2s, sem2r, sem3s, sem3r, sem4s, sem4r,
):
    x, yh, core, yl, z = place()
    me = yl * NZ + z
    y = yh * 2 + yl
    spot = lax.axis_index("dp")
    other = 1 - core
    twin = dev(x, yh, other, yl, z)
    hops = [(d, e) for d in (0, 1, 7, 2, 6, 3, 5, 4) for e in (0, 1) if (d, e) != (0, 0)]
    fs_at = [(lax.rem(z + d, NZ), lax.rem(yl + e, 2)) for d, e in hops]
    fs_from = [(lax.rem(z + NZ - d, NZ), lax.rem(yl + e, 2)) for d, e in hops]
    fs_dev = [dev(x, yh, core, b, a) for a, b in fs_at]
    dp_dev = [(lax.rem(spot + d, 32), me) for d in range(1, 32)]
    xs = [dev(lax.rem(x + d, NX), yh, core, yl, z) for d in range(1, NX)]
    xo = [dev(lax.rem(x + d, NX), yh, other, yl, z) for d in range(1, NX)]
    ys = [lax.rem(y + d, 8) for d in range(1, 8)]
    zs = [lax.rem(z + d, NZ) for d in range(1, NZ)]
    flip = dev(x, yh, core, 1 - yl, z)
    z_hops = (1, 7, 2, 6, 3, 5, 4)
    y_dev = [dev(x, n // 2, core, lax.rem(n, 2), z) for n in ys]
    z_dev = [dev(x, yh, core, yl, n) for n in zs]
    z_to = lambda d: dev(x, yh, core, yl, lax.rem(z + d, NZ))
    across = [dev(x, lax.rem(yh + d, NYH), core, 1 - yl, z) for d in range(1, NYH)]

    barrier = pltpu.get_barrier_semaphore()
    greeted = fs_dev + dp_dev + across
    for where in greeted:
        pl.semaphore_signal(barrier, inc=1, device_id=where, device_id_type=MESH)

    rows = pl.ds(pl.multiple_of(core * 32, 32), 32)
    loads = [
        pltpu.make_async_copy(down_ref.at[rows, :], par.at[core, me, :, pl.ds(0, 256)], load_sem.at[0]),
        pltpu.make_async_copy(up_ref.at[rows, :], par.at[core, me, :, pl.ds(256, HEAD)], load_sem.at[1]),
        pltpu.make_async_copy(gain_ref, gains.at[me], load_sem.at[2]),
    ]
    for copy in loads:
        copy.start()
    for kind, src in ((0, k_ref), (1, v_ref)):

        @pl.when(core == kind)
        def _():
            for g in range(GROUPS):
                pltpu.make_async_copy(src.at[:, pl.ds(g * HEAD, HEAD)], kv.at[kind, g, me], load_sem.at[3 + g]).start()

    bigs = [
        pltpu.make_async_copy(hidden_hbm, hidden, big_sem.at[0]),
        pltpu.make_async_copy(frozen_hbm, frozen, big_sem.at[1]),
        pltpu.make_async_copy(grad_hbm, grad, big_sem.at[2]),
    ]
    for copy in bigs:
        copy.start()

    place_row = lax.broadcasted_iota(jnp.int32, (RESP, 64), 1)
    resp = lax.broadcasted_iota(jnp.int32, (RESP, 64), 0)
    position = (spot * 64 + place_row) * FS + me
    limit = jnp.full((RESP, 64), lengths_ref[0], jnp.int32)
    for r in range(1, RESP):
        limit = jnp.where(resp == r, lengths_ref[r], limit)
    mine = jnp.sum(jnp.where(position < limit, tlr_ref[...], 0.0), axis=1, keepdims=True)
    tot1[me] = jnp.concatenate([jnp.broadcast_to(mine, (RESP, 128)), jnp.zeros((8 - RESP, 128), F32)], axis=0)

    for copy in loads:
        copy.wait()
    for g in range(GROUPS):
        pltpu.make_async_copy(k_ref.at[:, pl.ds(g * HEAD, HEAD)], kv.at[core, g, me], load_sem.at[3 + g]).wait()
    pl.semaphore_wait(barrier, len(greeted))

    sent = []
    for i, where in enumerate(fs_dev):
        sent.append(send(gains.at[me], gains.at[me], gs_sem.at[i], gr_sem.at[i], where))
    for i, d in enumerate(z_hops):
        sent.append(send(par.at[core, me], par.at[core, me], as_sem.at[GROUPS, i], ar_sem.at[GROUPS, i], z_to(d)))
    for i, where in enumerate(fs_dev):
        sent.append(send(tot1.at[me], tot1.at[me], t1s.at[i], t1r.at[i], where))
    for g in range(GROUPS):
        for i, d in enumerate(z_hops):
            sent.append(send(kv.at[core, g, me], kv.at[core, g, me], as_sem.at[g, i], ar_sem.at[g, i], z_to(d)))

    def landed(ref, sem):
        pltpu.make_async_remote_copy(
            src_ref=ref, dst_ref=ref, send_sem=sem, recv_sem=sem, device_id=twin, device_id_type=MESH
        ).wait_recv()

    def origin(i):
        a, b = fs_from[i]
        return b * NZ + a

    def plane(kind, chunk, b):
        shards = pl.ds(pl.multiple_of(b * NZ, NZ), NZ)
        return par.at[kind, shards] if chunk is None else kv.at[kind, chunk, shards]

    def slot(chunk):
        return GROUPS if chunk is None else chunk

    def pass_flip(chunk):
        at = slot(chunk)
        for i, d in enumerate(z_hops):
            shard = yl * NZ + lax.rem(z + NZ - d, NZ)
            landed(par.at[core, shard] if chunk is None else kv.at[core, chunk, shard], ar_sem.at[at, i])
        ref = plane(core, chunk, yl)
        send(ref, ref, fs_sem.at[at], fr_sem.at[at], flip)
        send(ref, ref, cs_sem.at[0, at], cr_sem.at[0, at], twin)

    def pass_twin(chunk):
        at = slot(chunk)
        ref = plane(core, chunk, 1 - yl)
        landed(ref, fr_sem.at[at])
        send(ref, ref, cs_sem.at[1, at], cr_sem.at[1, at], twin)

    def complete(chunk):
        at = slot(chunk)
        landed(plane(other, chunk, yl), cr_sem.at[0, at])
        landed(plane(other, chunk, 1 - yl), cr_sem.at[1, at])

    def left(chunk):
        at = slot(chunk)
        for sem, b in ((fs_sem.at[at], yl), (cs_sem.at[0, at], yl), (cs_sem.at[1, at], 1 - yl)):
            ref = plane(core, chunk, b)
            pltpu.make_async_remote_copy(
                src_ref=ref, dst_ref=ref, send_sem=sem, recv_sem=sem, device_id=twin, device_id_type=MESH
            ).wait_send()

    bigs[0].wait()
    square = jnp.zeros((ROWS, 256), F32)
    for f in range(FS):
        block = hidden[:, pl.ds(f * 256, 256)].astype(F32)
        square = square + block * block
    inv_ref[...] = lax.rsqrt(jnp.sum(square, axis=1, keepdims=True) * (1.0 / WIDTH) + EPS)
    low32[...] = jnp.zeros_like(low32)
    for i in range(len(fs_dev)):
        landed(gains.at[origin(i)], gr_sem.at[i])

    def norm_step(f, carry):
        gain = gains[f].astype(F32)
        for half in range(2):
            cols = pl.ds(pl.multiple_of(f * 256 + half * 128, 128), 128)
            normed[:, cols] = (hidden[:, cols].astype(F32) * inv_ref[...] * gain[half : half + 1]).astype(BF)
        return carry

    lax.fori_loop(0, FS, norm_step, 0)

    pass_flip(None)
    for i in range(len(fs_dev)):
        landed(tot1.at[origin(i)], t1r.at[i])
    total = tot1[0]
    for j in range(1, FS):
        total = total + tot1[j]
    tot2[spot] = total
    for d in range(31):
        sent.append(send(tot2.at[spot], tot2.at[spot], t2s.at[d], t2r.at[d], dp_dev[d]))
    pass_twin(None)
    pass_flip(0)
    complete(None)

    def low_step(f, carry):
        cols = pl.ds(pl.multiple_of(f * 256, 256), 256)
        low32[...] += mm(normed[:, cols], par[:, f, :, pl.ds(0, 256)].reshape(RANK, 256), NT)
        return carry

    lax.fori_loop(0, FS, low_step, 0)
    low_ref[...] = low32[...].astype(BF)
    glow_ref[...] = jnp.zeros_like(glow_ref)
    pass_twin(0)
    pass_flip(1)

    for d in range(31):
        landed(tot2.at[lax.rem(spot + 31 - d, 32)], t2r.at[d])
    total = tot2[0]
    for j in range(1, 32):
        total = total + tot2[j]
    seq_out[...] = total
    row = lax.broadcasted_iota(jnp.int32, (64, 1), 0)
    position = (spot * 64 + row) * FS + me
    for r in range(RESP):
        weight = 2.0 * (total[r : r + 1, 0:1] - (win_ref[r] - 0.5)) / RESP
        coef_ref[pl.ds(r * 64, 64), :] = jnp.where(position < lengths_ref[r], jnp.broadcast_to(weight, (64, 1)), 0.0) * SCALE
    bigs[1].wait()
    bigs[2].wait()

    def group_step(g, carry):
        @pl.when(g < GROUPS - 1)
        def _():
            pass_twin(g + 1)

        @pl.when(g < GROUPS - 2)
        def _():
            pass_flip(g + 2)

        complete(g)
        ups, queries, grads = [], [], []
        for a in range(PER):
            h = g * PER + a
            cols = pl.ds(pl.multiple_of(h * HEAD, HEAD), HEAD)
            ups.append(par[:, h, :, pl.ds(256, HEAD)].reshape(RANK, HEAD))
            queries.append((frozen[:, cols].astype(F32) + mm(low_ref[...], ups[a])).astype(BF))
            grads.append(grad[:, cols])
        keys = kv[0, g].reshape(PROMPT, HEAD)
        values = kv[1, g].reshape(PROMPT, HEAD)
        scores = mm(jnp.concatenate(queries, axis=0), keys, NT)
        top = jnp.max(scores, axis=1, keepdims=True)
        expo = jnp.exp2((scores - top) * (SCALE * math.log2(math.e)))
        row_total = jnp.sum(expo, axis=1, keepdims=True)
        weights = expo.astype(BF)
        grad_prob = mm(jnp.concatenate(grads, axis=0), values, NT)
        wide = weights.astype(F32)
        inner = jnp.sum(wide * grad_prob, axis=1, keepdims=True) / row_total
        grad_score = (wide * (grad_prob - inner)).astype(BF)
        coef = jnp.concatenate([coef_ref[...]] * PER, axis=0)
        grad_query = (mm(grad_score, keys) * (coef / row_total)).astype(BF)
        for a in range(PER):
            h = g * PER + a
            block = grad_query[a * ROWS : (a + 1) * ROWS]
            glow_ref[...] += mm(block, ups[a], NT)
            part[:, :, h, :, pl.ds(256, HEAD)] = mm(low_ref[...], block, TN).astype(BF).reshape(2, NX, 8, HEAD)
        return carry

    lax.fori_loop(0, GROUPS, group_step, 0)
    grad_low = glow_ref[...].astype(BF)

    pieces = 4
    size = FS // pieces
    swaps, steps = [], []

    def pass_x(p):
        blocks = pl.ds(p * size, size)
        swaps[p].wait_recv()
        s0[:, blocks] = (part[core, :, blocks].astype(F32) + r0[:, blocks].astype(F32)).astype(BF)
        for d in range(1, NX):
            steps.append(send(s0.at[lax.rem(x + d, NX), blocks], r1.at[d - 1, blocks], sem1s.at[p, d - 1], sem1r.at[p, d - 1], xs[d - 1]))

    for p in range(pieces):
        for f in range(p * size, (p + 1) * size):
            part[:, :, f, :, pl.ds(0, 256)] = mm(grad_low, normed[:, pl.ds(f * 256, 256)], TN).astype(BF).reshape(2, NX, 8, 256)
        blocks = pl.ds(p * size, size)
        swaps.append(send(part.at[other, :, blocks], r0.at[:, blocks], sem0s.at[p], sem0r.at[p], twin))
        if p:
            pass_x(p - 1)
    pass_x(pieces - 1)
    for copy in steps:
        copy.wait_recv()
    sum_x = s0[x].astype(F32)
    for d in range(1, NX):
        sum_x = sum_x + r1[d - 1].astype(F32)
    s1[...] = sum_x.astype(BF).reshape(2, NZ, 8, PCOLS)
    sent += swaps + steps
    steps = []
    for d in range(1, NZ):
        steps.append(send(s1.at[:, zs[d - 1]], r2.at[d - 1], sem2s.at[d - 1], sem2r.at[d - 1], z_dev[d - 1]))
    sum_z = s1[:, z].astype(F32)
    for d in range(1, NZ):
        steps[d - 1].wait_recv()
        sum_z = sum_z + r2[d - 1].astype(F32)
    s2[...] = sum_z.astype(BF)
    sent += steps
    steps = []
    for d in range(1, 8):
        steps.append(send(s2.at[lax.rem(ys[d - 1], 2)], r3.at[y], sem3s.at[d - 1], sem3r.at[d - 1], y_dev[d - 1]))
    r3[y] = s2[yl]
    for copy in steps:
        copy.wait_recv()
    sum_y = r3[0].astype(F32)
    for j in range(1, 8):
        sum_y = sum_y + r3[j].astype(F32)
    sent += steps
    s4[core, x] = sum_y
    steps = []
    for d, where in enumerate([twin] + xs + xo):
        steps.append(send(s4.at[core, x], s4.at[core, x], sem4s.at[d], sem4r.at[d], where))
    for copy in steps:
        copy.wait_recv()
    whole = s4[...].reshape(RANK, PCOLS)
    down_out[...] = whole[:, 0:256]
    up_out[...] = whole[:, 256:384]
    for copy in sent + steps:
        copy.wait_send()
    for chunk in [None] + list(range(GROUPS)):
        left(chunk)


def step(*args):
    any_ = pl.BlockSpec(memory_space=pl.ANY)
    vmem = pl.BlockSpec(memory_space=pltpu.VMEM)
    smem = pl.BlockSpec(memory_space=pltpu.SMEM)
    dma = pltpu.SemaphoreType.DMA
    wide = HEADS * HEAD
    return pl.pallas_call(
        step_kernel,
        out_shape=(
            jax.ShapeDtypeStruct((8, 128), F32),
            jax.ShapeDtypeStruct((RANK, 256), F32),
            jax.ShapeDtypeStruct((RANK, HEAD), F32),
        ),
        in_specs=[smem, smem, vmem] + [any_] * 8,
        out_specs=(vmem, vmem, vmem),
        scratch_shapes=[
            pltpu.VMEM((2, GROUPS, FS, 64, HEAD), BF),
            pltpu.VMEM((2, FS, 32, PCOLS), BF),
            pltpu.VMEM((FS, 2, 128), BF),
            pltpu.VMEM((ROWS, WIDTH), BF),
            pltpu.VMEM((ROWS, wide), BF),
            pltpu.VMEM((ROWS, wide), BF),
            pltpu.VMEM((ROWS, WIDTH), BF),
            pltpu.VMEM((ROWS, RANK), BF),
            pltpu.VMEM((ROWS, RANK), F32),
            pltpu.VMEM((ROWS, 1), F32),
            pltpu.VMEM((ROWS, 1), F32),
            pltpu.VMEM((ROWS, RANK), F32),
            pltpu.VMEM((FS, 8, 128), F32),
            pltpu.VMEM((32, 8, 128), F32),
            pltpu.VMEM((2, NX, FS, 8, PCOLS), BF),
            pltpu.VMEM((NX, FS, 8, PCOLS), BF),
            pltpu.VMEM((NX, FS, 8, PCOLS), BF),
            pltpu.VMEM((NX - 1, FS, 8, PCOLS), BF),
            pltpu.VMEM((2, NZ, 8, PCOLS), BF),
            pltpu.VMEM((NZ - 1, 2, 8, PCOLS), BF),
            pltpu.VMEM((2, 8, PCOLS), BF),
            pltpu.VMEM((8, 8, PCOLS), BF),
            pltpu.VMEM((2, NX, 8, PCOLS), F32),
            dma((7,)), dma((3,)),
            dma((GROUPS + 1, 7)), dma((GROUPS + 1, 7)), dma((GROUPS + 1,)), dma((GROUPS + 1,)),
            dma((15,)), dma((15,)),
            dma((2, GROUPS + 1)), dma((2, GROUPS + 1)),
            dma((15,)), dma((15,)), dma((31,)), dma((31,)),
            dma((4,)), dma((4,)), dma((4, 3)), dma((4, 3)),
            dma((7,)), dma((7,)), dma((7,)), dma((7,)), dma((7,)), dma((7,)),
        ],
        compiler_params=pltpu.CompilerParams(collective_id=0, has_side_effects=True, vmem_limit_bytes=60 * 1024 * 1024),
        name="step",
    )(*args)


def place_kernel(seq_ref, down_ref, up_ref, down_out, up_out, seq_out):
    down_out[...] = down_ref[...]
    up_out[...] = up_ref[...]
    for r in range(RESP):
        seq_out[r] = seq_ref[r, 0]


def place_outputs(seq, down, up):
    vmem = pl.BlockSpec(memory_space=pltpu.VMEM)
    smem = pl.BlockSpec(memory_space=pltpu.SMEM)
    return pl.pallas_call(
        place_kernel,
        out_shape=(
            jax.ShapeDtypeStruct((RANK, 256), F32),
            jax.ShapeDtypeStruct((RANK, HEAD), F32),
            jax.ShapeDtypeStruct((RESP,), F32),
        ),
        in_specs=[smem, vmem, vmem],
        out_specs=(vmem, vmem, smem),
        name="place_outputs",
    )(seq, down, up)


def body(
    hidden,
    frozen_query_rows,
    output_gradient,
    token_log_ratio,
    lengths,
    response_win_probability,
    cached_prompt_keys,
    cached_prompt_values,
    adapter_down_factor,
    adapter_up_factor,
    attention_norm_gain,
):
    seq, grad_down_t, grad_up = step(
        lengths,
        response_win_probability,
        token_log_ratio.reshape(RESP, 64),
        cached_prompt_keys,
        cached_prompt_values,
        adapter_down_factor.T,
        adapter_up_factor,
        attention_norm_gain.reshape(2, 128),
        hidden.reshape(ROWS, WIDTH),
        frozen_query_rows.reshape(ROWS, HEADS * HEAD),
        output_gradient.reshape(ROWS, HEADS * HEAD),
    )
    grad_down_t, grad_up, seq_ratio = place_outputs(seq, grad_down_t, grad_up)
    return grad_down_t.T, grad_up, seq_ratio


def solution(mesh):
    in_specs = (
        P(None, "dp", "fsdp", None),
        P(None, "dp", "fsdp", None),
        P(None, "dp", "fsdp", None),
        P(None, "dp", "fsdp"),
        P(),
        P(),
        P("fsdp", None),
        P("fsdp", None),
        P("fsdp", None),
        P(None, "fsdp"),
        P("fsdp"),
    )
    out_specs = (P("fsdp", None), P(None, "fsdp"), P())
    return jax.shard_map(body, mesh=mesh, in_specs=in_specs, out_specs=out_specs, check_vma=False)
```
